32 devices in a mesh: section: 4 (over z), ctx: 8 (over y, x, core).
Axes of the slice: x: 2, y: 2, z: 4, core: 2. Of those that a mesh axis runs over, the one named last changes fastest.
Arguments:
- query: bfloat16 [4, 3072, 3072], P('section', 'ctx'), may hold values from -200 to 200
- key: bfloat16 [4, 3072, 3072], P('section', 'ctx'), may hold values from -6 to 6
- value: bfloat16 [4, 3072, 3072], P('section', 'ctx'), may hold values from -6 to 6
- out_grad: bfloat16 [4, 3072, 3072], P('section', 'ctx'), may hold values from -6 to 6
- tile_mask: int32 [16, 8], P('ctx'), may hold values from 0 to 1, as said below
Outputs:
- key_grad: bfloat16 [4, 3072, 3072], P('section', 'ctx')
- value_grad: bfloat16 [4, 3072, 3072], P('section', 'ctx')
- upstream: bfloat16 [4, 3072, 3072], P('section', 'ctx')
The draws below stay inside these ranges and needn't reach their ends.
Inputs may be any that keep to these rules, and one draw needn't show every extreme that they name: `tile_mask`: every query tile a reads the key tile a // 2 of its own image rows; the share of ones differs from one pair of query tiles to the next.
All inputs are finite; a program needn't handle non-finite values.
Results may differ from the reference program's by a relative error of at most 0.014.
The reference program's roundings to bfloat16 on the way count: a program that leaves them out, or rounds other values in their place, can miss the bound.
Values may be sent and summed in bfloat16 or wider, within the bound.
A program may use at most 256 MiB of HBM per device.

```python
import jax
import jax.numpy as jnp
from jax import lax

H = 24
HD = 128
IMG_W = 192
C = 3072
TOK_DEV = 384
POOL_DEV = 96
TOKENS = 3072
SECTIONS = 4
QTILES = 16
KTILES = 8


def draw_query(key, part):
    base = jax.random.normal(jax.random.fold_in(key, 11), (SECTIONS, TOKENS, C), jnp.float32)
    return jnp.clip(base, -200.0, 200.0).astype(jnp.bfloat16)


def draw_tile_mask(key, part):
    qtile = jnp.arange(QTILES, dtype=jnp.int32)
    ktile = jnp.arange(KTILES, dtype=jnp.int32)
    owner = qtile // 2
    level = 1 + owner * 5 % 7
    coins = jax.random.randint(jax.random.fold_in(key, 21), (QTILES, KTILES), 0, 8)
    chosen = coins < level[:, None]
    own = ktile[None, :] == owner[:, None]
    return jnp.where(chosen | own, 1, 0).astype(jnp.int32)


def block_scale(own_key, dims, cuts, smallest, high):
    factor_of, own = 1.0, jax.random.fold_in(own_key, 6)
    for axis_at, blocks in cuts:
        steps = jnp.exp(jax.random.uniform(jax.random.fold_in(own, axis_at), (blocks,), jnp.float32, smallest / len(cuts), high / len(cuts)))
        factor_of = factor_of * jnp.repeat(steps, dims[axis_at] // blocks).reshape([-1 if axis == axis_at else 1 for axis in range(len(dims))])
    return factor_of


def normal_values(rng, dims, deviation, reach, cuts=(), held_as=jnp.bfloat16):
    result = deviation * jax.random.normal(rng, dims, jnp.float32)
    if cuts:
        result = result * block_scale(rng, dims, cuts, -0.22, 0.18)
    return jnp.clip(result, -reach, reach).astype(held_as)


def setup_inputs(seed: int = 0) -> dict:
    arg_keys = jax.random.split(jax.random.key(seed), 6)
    return {
        "query": draw_query(jax.random.fold_in(arg_keys[5], 71), 0),
        "key": normal_values(arg_keys[1], (SECTIONS, TOKENS, C), 1.0, 6.0, ((0, 4), (1, 8))),
        "value": normal_values(arg_keys[2], (SECTIONS, TOKENS, C), 1.0, 6.0, ((0, 4), (1, 8))),
        "out_grad": normal_values(arg_keys[3], (SECTIONS, TOKENS, C), 1.0, 6.0, ((0, 4), (1, 8))),
        "tile_mask": draw_tile_mask(jax.random.fold_in(arg_keys[5], 71), 0),
    }


def pool_rows(data):
    rows = data.shape[0] // IMG_W
    grid = data.astype(jnp.float32).reshape(rows // 2, 2, IMG_W // 2, 2, data.shape[1])
    return grid.mean(axis=(1, 3)).reshape(-1, data.shape[1]).astype(jnp.bfloat16)


def unpool_rows(pooled):
    rows = pooled.shape[0] // (IMG_W // 2)
    grid = (pooled / 4.0).reshape(rows, 1, IMG_W // 2, 1, pooled.shape[1])
    grid = jnp.broadcast_to(grid, (rows, 2, IMG_W // 2, 2, pooled.shape[1]))
    return grid.reshape(-1, pooled.shape[1]).astype(jnp.bfloat16)


def head_backward(qhead, khead, vhead, dhead, allowed):
    scale = 1.0 / (HD ** 0.5)
    scores = jnp.dot(qhead, khead.T, preferred_element_type=jnp.float32) * scale
    scores = jnp.where(allowed, scores, -1e30)
    top = jnp.max(scores, axis=1, keepdims=True)
    expo = jnp.exp(scores - top)
    probs = expo / jnp.sum(expo, axis=1, keepdims=True)
    probs_low = probs.astype(jnp.bfloat16)
    attended = jnp.dot(probs_low, vhead, preferred_element_type=jnp.float32)
    delta = jnp.sum(dhead.astype(jnp.float32) * attended, axis=1, keepdims=True)
    dprob = jnp.dot(dhead, vhead.T, preferred_element_type=jnp.float32)
    score_grad = (probs * (dprob - delta) * scale).astype(jnp.bfloat16)
    qgrad = jnp.dot(score_grad, khead, preferred_element_type=jnp.float32).astype(jnp.bfloat16)
    count = qhead.shape[0] // TOK_DEV
    sg = score_grad.astype(jnp.float32).reshape(count, TOK_DEV, -1)
    pl = probs_low.astype(jnp.float32).reshape(count, TOK_DEV, -1)
    qf = qhead.astype(jnp.float32).reshape(count, TOK_DEV, HD)
    df = dhead.astype(jnp.float32).reshape(count, TOK_DEV, HD)
    kterm = jnp.einsum("ntk,ntd->nkd", sg, qf).astype(jnp.bfloat16).astype(jnp.float32)
    vterm = jnp.einsum("ntk,ntd->nkd", pl, df).astype(jnp.bfloat16).astype(jnp.float32)
    return qgrad, jnp.sum(kterm, axis=0), jnp.sum(vterm, axis=0)


def section_backward(query, key, value, out_grad, allowed):
    pooled_key = pool_rows(key)
    pooled_value = pool_rows(value)
    tokens = query.shape[0]
    def per_head(index):
        start = index * HD
        qh = lax.dynamic_slice_in_dim(query, start, HD, 1)
        kh = lax.dynamic_slice_in_dim(pooled_key, start, HD, 1)
        vh = lax.dynamic_slice_in_dim(pooled_value, start, HD, 1)
        dh = lax.dynamic_slice_in_dim(out_grad, start, HD, 1)
        return head_backward(qh, kh, vh, dh, allowed)
    qgrad, kgrad, vgrad = lax.map(per_head, jnp.arange(H, dtype=jnp.int32))
    qgrad = jnp.transpose(qgrad, (1, 0, 2)).reshape(tokens, H * HD)
    kgrad = jnp.transpose(kgrad, (1, 0, 2)).reshape(-1, H * HD)
    vgrad = jnp.transpose(vgrad, (1, 0, 2)).reshape(-1, H * HD)
    return qgrad, unpool_rows(kgrad), unpool_rows(vgrad)


def reference(query, key, value, out_grad, tile_mask):
    rows_mask = jnp.repeat(tile_mask, IMG_W, axis=0)
    allowed = jnp.repeat(rows_mask, POOL_DEV, axis=1) > 0
    def one_section(items):
        return section_backward(items[0], items[1], items[2], items[3], allowed)
    qgrad, kgrad, vgrad = lax.map(one_section, (query, key, value, out_grad))
    upstream = jnp.concatenate([qgrad[1:], jnp.zeros_like(qgrad[:1])], axis=0)
    return kgrad, vgrad, upstream
```

```python
import functools

import jax
import jax.numpy as jnp
from jax import lax
from jax.experimental import pallas as pl
from jax.experimental.pallas import tpu as pltpu
from jax.sharding import PartitionSpec as P

HD = 128
MESH = pl.DeviceIdType.MESH
LOG2E = 1.4426950408889634


def dot(a, b, dims):
    return lax.dot_general(a, b, (dims, ((), ())), preferred_element_type=jnp.float32)


def kernel(
    sections, count, groups, wide,
    q_hbm, k_hbm, v_hbm, d_hbm, bias_hbm,
    kg_hbm, vg_hbm, up_hbm,
    kin, pooled, kv, qd, bias, terms, arrived, dq,
    in_sem, own_sem, own_bias_sem, swap_send, swap_recv, bias_sems,
    kv_send, kv_recv, term_send, term_recv, dq_send, dq_recv, out_sem,
):
    tokens = qd.shape[3]
    row_len = tokens // 2
    pool = pooled.shape[3]
    section = lax.axis_index("section")
    me = lax.axis_index("ctx")
    core = lax.rem(me, 2)
    chip_first = me - core
    partner = chip_first + 1 - core

    def columns(half, g):
        return pl.ds(pl.multiple_of((half * groups + g) * wide, wide), wide)

    def in_copy(which, half, g):
        src = (k_hbm, v_hbm)[which]
        return pltpu.make_async_copy(
            src.at[0, :, columns(half, g)], kin.at[which, :, columns(half, g)], in_sem.at[which, half, g]
        )

    def own_copy(which, g):
        src = (q_hbm, d_hbm)[which]
        return pltpu.make_async_copy(src.at[0, :, columns(core, g)], qd.at[g, which, core], own_sem.at[which, g])

    def own_bias():
        return pltpu.make_async_copy(bias_hbm, bias.at[core], own_bias_sem)

    @pl.loop(0, groups)
    def _(g):
        for which in range(2):
            for half in range(2):
                in_copy(which, half, g).start()

    @pl.loop(0, groups)
    def _(g):
        for which in range(2):
            own_copy(which, g).start()

    own_bias().start()

    barrier = pltpu.get_barrier_semaphore()
    for step in range(1, count):
        pl.semaphore_signal(
            barrier, inc=1, device_id=(section, lax.rem(me + step, count)), device_id_type=MESH
        )

    @pl.when(section > 0)
    def _():
        for c in range(2):
            pl.semaphore_signal(barrier, inc=1, device_id=(section - 1, chip_first + c), device_id_type=MESH)

    @pl.when(section < sections - 1)
    def _():
        for c in range(2):
            pl.semaphore_signal(barrier, inc=1, device_id=(section + 1, chip_first + c), device_id_type=MESH)

    edges = jnp.where(section > 0, 2, 0) + jnp.where(section < sections - 1, 2, 0)
    pl.semaphore_wait(barrier, count - 1 + edges)

    def swap(which, g):
        src = (q_hbm, d_hbm)[which]
        return pltpu.make_async_remote_copy(
            src_ref=src.at[0, :, columns(1 - core, g)],
            dst_ref=qd.at[g, which, core],
            send_sem=swap_send.at[which, g],
            recv_sem=swap_recv.at[which, g],
            device_id=(section, partner),
            device_id_type=MESH,
        )

    def swap_bias():
        return pltpu.make_async_remote_copy(
            src_ref=bias_hbm,
            dst_ref=bias.at[core],
            send_sem=bias_sems.at[0],
            recv_sem=bias_sems.at[1],
            device_id=(section, partner),
            device_id_type=MESH,
        )

    swap_bias().start()

    @pl.loop(0, groups)
    def _(g):
        for which in range(2):
            swap(which, g).start()

    def kv_out(g, peer):
        return pltpu.make_async_remote_copy(
            src_ref=pooled.at[lax.rem(peer, 2), g],
            dst_ref=kv.at[g, me],
            send_sem=kv_send.at[g, peer],
            recv_sem=kv_recv.at[g, me],
            device_id=(section, peer),
            device_id_type=MESH,
        )

    def kv_in(g, peer):
        return pltpu.make_async_remote_copy(
            src_ref=pooled.at[core, g],
            dst_ref=kv.at[g, peer],
            send_sem=kv_send.at[g, peer],
            recv_sem=kv_recv.at[g, peer],
            device_id=(section, peer),
            device_id_type=MESH,
        )

    def pool_matrix(shape, token_dim, value):
        token = lax.broadcasted_iota(jnp.int32, shape, token_dim)
        token = jnp.where(token >= row_len, token - row_len, token)
        cell = lax.broadcasted_iota(jnp.int32, shape, 1 - token_dim)
        return jnp.where((token >> 1) == cell, value, 0.0).astype(jnp.bfloat16)

    @pl.loop(0, groups)
    def _(g):
        mean = pool_matrix((pool, tokens), 1, 0.25)
        for half in range(2):
            for which in range(2):
                in_copy(which, half, g).wait()
                block = dot(mean, kin[which, :, columns(half, g)], ((1,), (0,)))
                pooled[half, g, which] = block.astype(jnp.bfloat16)
        kv[g, me] = pooled[core, g]

        @pl.loop(1, count)
        def _(step):
            kv_out(g, lax.rem(me + step, count)).start()

    def term_out(g, peer):
        return pltpu.make_async_remote_copy(
            src_ref=terms.at[g, peer],
            dst_ref=arrived.at[g, me],
            send_sem=term_send.at[g, peer],
            recv_sem=term_recv.at[g, me],
            device_id=(section, peer),
            device_id_type=MESH,
        )

    def term_in(g, peer):
        return pltpu.make_async_remote_copy(
            src_ref=terms.at[g, peer],
            dst_ref=arrived.at[g, peer],
            send_sem=term_send.at[g, peer],
            recv_sem=term_recv.at[g, peer],
            device_id=(section, peer),
            device_id_type=MESH,
        )

    def dq_out(g, c):
        return pltpu.make_async_remote_copy(
            src_ref=dq.at[g, c],
            dst_ref=up_hbm.at[0, :, columns(core, g)],
            send_sem=dq_send.at[g, c],
            recv_sem=dq_recv.at[g, core],
            device_id=(section - 1, chip_first + c),
            device_id_type=MESH,
        )

    def dq_in(g, c):
        return pltpu.make_async_remote_copy(
            src_ref=dq.at[g, c],
            dst_ref=up_hbm.at[0, :, columns(c, g)],
            send_sem=dq_send.at[g, c],
            recv_sem=dq_recv.at[g, c],
            device_id=(section + 1, chip_first + c),
            device_id_type=MESH,
        )

    own_bias().wait()
    swap_bias().wait()
    scale = 1.0 / HD**0.5

    @pl.loop(0, groups)
    def _(g):
        for which in range(2):
            own_copy(which, g).wait()
            swap(which, g).wait()

        @pl.loop(1, count)
        def _(step):
            kv_in(g, lax.rem(me + step, count)).wait_recv()

        for h in range(wide // HD):
            hs = slice(h * HD, (h + 1) * HD)
            k2 = kv[g, :, 0, :, hs].reshape(count * pool, HD)
            v2 = kv[g, :, 1, :, hs].reshape(count * pool, HD)
            dk = dv = None
            for c in range(2):
                qc = qd[g, 0, c, :, hs]
                dc = qd[g, 1, c, :, hs]
                scores = dot(k2, qc, ((1,), (1,))).reshape(count, pool, tokens)
                scores = (scores + bias[c][:, None, :]).reshape(count * pool, tokens)
                top = jnp.max(scores, axis=0, keepdims=True)
                expo = jnp.exp2((scores - top) * (scale * LOG2E))
                probs = expo * (1.0 / jnp.sum(expo, axis=0, keepdims=True))
                low = probs.astype(jnp.bfloat16)
                dprob = dot(v2, dc, ((1,), (1,)))
                delta = jnp.sum(low.astype(jnp.float32) * dprob, axis=0, keepdims=True)
                sgrad = (probs * (dprob - delta) * scale).astype(jnp.bfloat16)
                dkc = dot(sgrad, qc, ((1,), (0,)))
                dvc = dot(low, dc, ((1,), (0,)))
                dk = dkc if dk is None else dk + dkc
                dv = dvc if dv is None else dv + dvc
                dq[g, c, :, hs] = dot(k2, sgrad, ((0,), (0,))).T.astype(jnp.bfloat16)
            terms[g, :, 0, :, hs] = dk.astype(jnp.bfloat16).reshape(count, pool, HD)
            terms[g, :, 1, :, hs] = dv.astype(jnp.bfloat16).reshape(count, pool, HD)

        @pl.loop(1, count)
        def _(step):
            term_out(g, lax.rem(me + step, count)).start()

        @pl.when(section > 0)
        def _():
            for c in range(2):
                dq_out(g, c).start()

        arrived[g, me] = terms[g, me]

    def grad_out(which, half, g):
        dst = (kg_hbm, vg_hbm)[which]
        return pltpu.make_async_copy(
            kin.at[which, :, columns(half, g)], dst.at[0, :, columns(half, g)], out_sem.at[which, half, g]
        )

    @pl.loop(0, groups)
    def _(g):
        @pl.loop(1, count)
        def _(step):
            term_in(g, lax.rem(me + step, count)).wait_recv()

        spread = pool_matrix((tokens, pool), 0, 1.0)
        for half in range(2):
            for which in range(2):
                total = arrived[g, half, which].astype(jnp.float32)
                for peer in range(half + 2, count, 2):
                    total = total + arrived[g, peer, which].astype(jnp.float32)
                grad = (total / 4.0).astype(jnp.bfloat16)
                kin[which, :, columns(half, g)] = dot(spread, grad, ((1,), (0,))).astype(jnp.bfloat16)
                grad_out(which, half, g).start()

    @pl.when(section == sections - 1)
    def _():
        qd[0, 0, 0] = jnp.zeros((tokens, wide), jnp.bfloat16)

        def zero_out(g, half):
            return pltpu.make_async_copy(qd.at[0, 0, 0], up_hbm.at[0, :, columns(half, g)], dq_recv.at[g, half])

        for half in range(2):
            for g in range(groups):
                zero_out(g, half).start()
        for half in range(2):
            for g in range(groups):
                zero_out(g, half).wait()

    @pl.loop(0, groups)
    def _(g):
        for which in range(2):
            for half in range(2):
                grad_out(which, half, g).wait()

        @pl.loop(1, count)
        def _(step):
            peer = lax.rem(me + step, count)
            kv_out(g, peer).wait_send()
            term_out(g, peer).wait_send()

        @pl.when(section > 0)
        def _():
            for c in range(2):
                dq_out(g, c).wait_send()

        @pl.when(section < sections - 1)
        def _():
            for c in range(2):
                dq_in(g, c).wait_recv()


def shards(query, key, value, out_grad, tile_mask):
    _, tokens, width = query.shape
    sections = lax.axis_size("section")
    count = lax.axis_size("ctx")
    pool = tokens // 4
    half_heads = width // HD // 2
    per_group = 2 if half_heads % 2 == 0 else 1
    groups = half_heads // per_group
    wide = per_group * HD
    allowed = jnp.repeat(tile_mask.T, tokens // 2, axis=1) > 0
    bias = jnp.where(allowed, 0.0, -1e30).astype(jnp.float32)
    any_spec = pl.BlockSpec(memory_space=pltpu.HBM)
    dma = pltpu.SemaphoreType.DMA
    low = jnp.bfloat16
    whole = jax.ShapeDtypeStruct(query.shape, low)
    return pl.pallas_call(
        functools.partial(kernel, sections, count, groups, wide),
        out_shape=(whole, whole, whole),
        in_specs=[any_spec] * 5,
        out_specs=(any_spec,) * 3,
        scratch_shapes=[
            pltpu.VMEM((2, tokens, width), low),
            pltpu.VMEM((2, groups, 2, pool, wide), low),
            pltpu.VMEM((groups, count, 2, pool, wide), low),
            pltpu.VMEM((groups, 2, 2, tokens, wide), low),
            pltpu.VMEM((2,) + bias.shape, jnp.float32),
            pltpu.VMEM((groups, count, 2, pool, wide), low),
            pltpu.VMEM((groups, count, 2, pool, wide), low),
            pltpu.VMEM((groups, 2, tokens, wide), low),
            dma((2, 2, groups)),
            dma((2, groups)),
            dma,
            dma((2, groups)),
            dma((2, groups)),
            dma((2,)),
            dma((groups, count)),
            dma((groups, count)),
            dma((groups, count)),
            dma((groups, count)),
            dma((groups, 2)),
            dma((groups, 2)),
            dma((2, 2, groups)),
        ],
        compiler_params=pltpu.CompilerParams(
            collective_id=0, has_side_effects=True, vmem_limit_bytes=60 * 1024 * 1024
        ),
    )(query, key, value, out_grad, bias)


def solution(mesh):
    spec = P("section", "ctx", None)
    return jax.shard_map(
        shards,
        mesh=mesh,
        in_specs=(spec, spec, spec, spec, P("ctx", None)),
        out_specs=(spec, spec, spec),
        check_vma=False,
    )
```

```python
import functools

import jax
import jax.numpy as jnp
from jax import lax
from jax.experimental import pallas as pl
from jax.experimental.pallas import tpu as pltpu
from jax.sharding import PartitionSpec as P

HD = 128
MESH = pl.DeviceIdType.MESH
LOG2E = 1.4426950408889634
AHEAD = 2


def dot(a, b, dims):
    return lax.dot_general(a, b, (dims, ((), ())), preferred_element_type=jnp.float32)


def kernel(
    sections, count, groups, wide,
    q_hbm, k_hbm, v_hbm, d_hbm, mask_hbm,
    pg_hbm, up_hbm,
    kin, pooled, kv, qd, mask, bias, terms, arrived, relayed, dq, grads,
    in_sem, own_sem, mask_sem, swap_send, swap_recv, bias_sems,
    kv_send, kv_recv, pass_send, pass_recv, term_send, term_recv, relay_send, relay_recv,
    dq_send, dq_recv, out_sem,
):
    tokens = qd.shape[3]
    row_len = tokens // 2
    pool = pooled.shape[3]
    section = lax.axis_index("section")
    me = lax.axis_index("ctx")
    core = lax.rem(me, 2)
    chip_first = me - core
    partner = chip_first + 1 - core
    relay = count == 8
    across = lax.rem(me // 2, 2)
    beside_x = chip_first + 2 - 4 * across
    beside_y = chip_first + 4 - 8 * (me // 4)
    corner = 2 * (count // 2 - 1) - chip_first

    def columns(half, g):
        return pl.ds(pl.multiple_of((half * groups + g) * wide, wide), wide)

    def in_copy(which, half, g):
        src = (k_hbm, v_hbm)[which]
        return pltpu.make_async_copy(
            src.at[0, :, columns(half, g)], kin.at[which, :, columns(half, g)], in_sem.at[which, half, g]
        )

    def own_copy(which, g):
        src = (q_hbm, d_hbm)[which]
        return pltpu.make_async_copy(src.at[0, :, columns(core, g)], qd.at[g, which, core], own_sem.at[which, g])

    def own_mask():
        return pltpu.make_async_copy(mask_hbm, mask, mask_sem)

    @pl.loop(0, groups)
    def _(g):
        for which in range(2):
            for half in range(2):
                in_copy(which, half, g).start()

    @pl.loop(0, groups)
    def _(g):
        for which in range(2):
            own_copy(which, g).start()

    own_mask().start()

    own_mask().wait()
    tile = lax.broadcasted_iota(jnp.int32, (2, tokens), 0)
    token = lax.broadcasted_iota(jnp.int32, (2, tokens), 1)
    inside = jnp.where((token >= row_len) == (tile == 1), 1.0, 0.0)
    reads = dot(mask[...].astype(jnp.float32), inside, ((0,), (0,)))
    bias[core] = jnp.where(reads > 0.5, 0.0, -1e30)

    barrier = pltpu.get_barrier_semaphore()
    for step in range(1, count):
        pl.semaphore_signal(
            barrier, inc=1, device_id=(section, lax.rem(me + step, count)), device_id_type=MESH
        )

    @pl.when(section > 0)
    def _():
        for c in range(2):
            pl.semaphore_signal(barrier, inc=1, device_id=(section - 1, chip_first + c), device_id_type=MESH)

    @pl.when(section < sections - 1)
    def _():
        for c in range(2):
            pl.semaphore_signal(barrier, inc=1, device_id=(section + 1, chip_first + c), device_id_type=MESH)

    edges = jnp.where(section > 0, 2, 0) + jnp.where(section < sections - 1, 2, 0)
    pl.semaphore_wait(barrier, count - 1 + edges)

    def swap(which, g):
        src = (q_hbm, d_hbm)[which]
        return pltpu.make_async_remote_copy(
            src_ref=src.at[0, :, columns(1 - core, g)],
            dst_ref=qd.at[g, which, core],
            send_sem=swap_send.at[which, g],
            recv_sem=swap_recv.at[which, g],
            device_id=(section, partner),
            device_id_type=MESH,
        )

    def swap_bias():
        return pltpu.make_async_remote_copy(
            src_ref=bias.at[core],
            dst_ref=bias.at[core],
            send_sem=bias_sems.at[0],
            recv_sem=bias_sems.at[1],
            device_id=(section, partner),
            device_id_type=MESH,
        )

    def kv_out(g, peer):
        return pltpu.make_async_remote_copy(
            src_ref=pooled.at[lax.rem(peer, 2), g],
            dst_ref=kv.at[g, me],
            send_sem=kv_send.at[g, peer],
            recv_sem=kv_recv.at[g, me],
            device_id=(section, peer),
            device_id_type=MESH,
        )

    def kv_in(g, peer):
        return pltpu.make_async_remote_copy(
            src_ref=pooled.at[core, g],
            dst_ref=kv.at[g, peer],
            send_sem=kv_send.at[g, peer],
            recv_sem=kv_recv.at[g, peer],
            device_id=(section, peer),
            device_id_type=MESH,
        )

    def pool_matrix(shape, token_dim, value):
        token = lax.broadcasted_iota(jnp.int32, shape, token_dim)
        token = jnp.where(token >= row_len, token - row_len, token)
        cell = lax.broadcasted_iota(jnp.int32, shape, 1 - token_dim)
        return jnp.where((token >> 1) == cell, value, 0.0).astype(jnp.bfloat16)

    def passed(g, which, j):
        src = ((beside_x, beside_y)[which]) + j
        dst = ((beside_y, beside_x)[which]) + core
        return pltpu.make_async_remote_copy(
            src_ref=kv.at[g, src, which],
            dst_ref=kv.at[g, src, which],
            send_sem=pass_send.at[g, which, j],
            recv_sem=pass_recv.at[g, which, j],
            device_id=(section, dst),
            device_id_type=MESH,
        )

    def each_peer(act):
        if relay:
            for j in range(2):
                act(beside_x + j)
                act(beside_y + j)
            act(partner)
        else:
            @pl.loop(1, count)
            def _(step):
                act(lax.rem(me + step, count))

    def pool_group(g):
        mean = pool_matrix((pool, tokens), 1, 0.25)
        for half in range(2):
            for which in range(2):
                in_copy(which, half, g).wait()
                block = dot(mean, kin[which, :, columns(half, g)], ((1,), (0,)))
                pooled[half, g, which] = block.astype(jnp.bfloat16)
        kv[g, me] = pooled[core, g]

    def send_group(g):
        each_peer(lambda peer: kv_out(g, peer).start())
        for which in range(2):
            swap(which, g).start()

    def pass_group(g):
        each_peer(lambda peer: kv_in(g, peer).wait_recv())
        if relay:
            for which in range(2):
                for j in range(2):
                    passed(g, which, j).start()

    ahead = min(AHEAD, groups)
    swap_bias().start()
    for g in range(ahead):
        pool_group(g)
        send_group(g)

    @pl.loop(ahead, groups)
    def _(g):
        pool_group(g)

    pass_group(0)

    def term_out(g, peer, which):
        return pltpu.make_async_remote_copy(
            src_ref=terms.at[g, peer, which],
            dst_ref=arrived.at[g, me, which],
            send_sem=term_send.at[g, peer, which],
            recv_sem=term_recv.at[g, me, which],
            device_id=(section, peer),
            device_id_type=MESH,
        )

    def term_in(g, peer, which):
        return pltpu.make_async_remote_copy(
            src_ref=terms.at[g, peer, which],
            dst_ref=arrived.at[g, peer, which],
            send_sem=term_send.at[g, peer, which],
            recv_sem=term_recv.at[g, peer, which],
            device_id=(section, peer),
            device_id_type=MESH,
        )

    def relay_out(g, which, j):
        return pltpu.make_async_remote_copy(
            src_ref=terms.at[g, corner + j, which],
            dst_ref=relayed.at[g, which, j],
            send_sem=relay_send.at[g, which, j],
            recv_sem=relay_recv.at[g, which, j],
            device_id=(section, ((beside_x, beside_y)[which]) + core),
            device_id_type=MESH,
        )

    def combine(g):
        for which in range(2):
            for j in range(2):
                relay_out(g, which, j).wait_recv()
                peer = ((beside_y, beside_x)[which]) + j
                both = terms[g, peer, which].astype(jnp.float32) + relayed[g, which, j].astype(jnp.float32)
                terms[g, peer, which] = both.astype(jnp.bfloat16)
                term_out(g, peer, which).start()

    def send_terms(g):
        if relay:
            for which in range(2):
                for j in range(2):
                    relay_out(g, which, j).start()
            for which in range(2):
                for j in range(2):
                    term_out(g, ((beside_x, beside_y)[which]) + j, which).start()
                term_out(g, partner, which).start()
        else:
            @pl.loop(1, count)
            def _(step):
                for which in range(2):
                    term_out(g, lax.rem(me + step, count), which).start()

    def dq_out(g, c):
        return pltpu.make_async_remote_copy(
            src_ref=dq.at[g, c],
            dst_ref=up_hbm.at[0, :, columns(core, g)],
            send_sem=dq_send.at[g, c],
            recv_sem=dq_recv.at[g, core],
            device_id=(section - 1, chip_first + c),
            device_id_type=MESH,
        )

    def dq_in(g, c):
        return pltpu.make_async_remote_copy(
            src_ref=dq.at[g, c],
            dst_ref=up_hbm.at[0, :, columns(c, g)],
            send_sem=dq_send.at[g, c],
            recv_sem=dq_recv.at[g, c],
            device_id=(section + 1, chip_first + c),
            device_id_type=MESH,
        )

    swap_bias().wait()
    scale = 1.0 / HD**0.5

    @pl.loop(0, groups)
    def _(g):
        for which in range(2):
            own_copy(which, g).wait()
            swap(which, g).wait()

        if relay:
            for which in range(2):
                for j in range(2):
                    passed(g, which, j).wait_recv()

        @pl.when(g + ahead < groups)
        def _():
            send_group(g + ahead)

        for h in range(wide // HD):
            hs = slice(h * HD, (h + 1) * HD)
            k2 = kv[g, :, 0, :, hs].reshape(count * pool, HD)
            v2 = kv[g, :, 1, :, hs].reshape(count * pool, HD)
            dk = dv = None
            for c in range(2):
                qc = qd[g, 0, c, :, hs]
                dc = qd[g, 1, c, :, hs]
                scores = dot(k2, qc, ((1,), (1,))).reshape(count, pool, tokens)
                scores = (scores + bias[c][:, None, :]).reshape(count * pool, tokens)
                top = jnp.max(scores, axis=0, keepdims=True)
                expo = jnp.exp2((scores - top) * (scale * LOG2E))
                probs = expo * (1.0 / jnp.sum(expo, axis=0, keepdims=True))
                low = probs.astype(jnp.bfloat16)
                dprob = dot(v2, dc, ((1,), (1,)))
                delta = jnp.sum(low.astype(jnp.float32) * dprob, axis=0, keepdims=True)
                sgrad = (probs * (dprob - delta) * scale).astype(jnp.bfloat16)
                dkc = dot(sgrad, qc, ((1,), (0,)))
                dvc = dot(low, dc, ((1,), (0,)))
                dk = dkc if dk is None else dk + dkc
                dv = dvc if dv is None else dv + dvc
                dq[g, c, :, hs] = dot(k2, sgrad, ((0,), (0,))).T.astype(jnp.bfloat16)
            terms[g, :, 0, :, hs] = dk.astype(jnp.bfloat16).reshape(count, pool, HD)
            terms[g, :, 1, :, hs] = dv.astype(jnp.bfloat16).reshape(count, pool, HD)
            if h == 0:
                @pl.when(g + 1 < groups)
                def _():
                    pass_group(g + 1)

                if relay:
                    @pl.when(g > 0)
                    def _():
                        combine(g - 1)

        send_terms(g)

        @pl.when(section > 0)
        def _():
            for c in range(2):
                dq_out(g, c).start()

        arrived[g, me] = terms[g, me]

    if relay:
        combine(groups - 1)

    def grad_out(half, g):
        return pltpu.make_async_copy(grads.at[half, g], pg_hbm.at[:, :, columns(half, g)], out_sem.at[half, g])

    @pl.loop(0, groups)
    def _(g):
        each_peer(lambda peer: [term_in(g, peer, which).wait_recv() for which in range(2)])
        for half in range(2):
            if relay:
                peers = [chip_first + half, beside_x + half, beside_y + half]
            else:
                peers = range(half, count, 2)
            for which in range(2):
                total = sum(arrived[g, peer, which].astype(jnp.float32) for peer in peers)
                grads[half, g, which] = (total / 4.0).astype(jnp.bfloat16)
            grad_out(half, g).start()

    @pl.when(section == sections - 1)
    def _():
        qd[0, 0, 0] = jnp.zeros((tokens, wide), jnp.bfloat16)

        def zero_out(g, half):
            return pltpu.make_async_copy(qd.at[0, 0, 0], up_hbm.at[0, :, columns(half, g)], dq_recv.at[g, half])

        for half in range(2):
            for g in range(groups):
                zero_out(g, half).start()
        for half in range(2):
            for g in range(groups):
                zero_out(g, half).wait()

    @pl.loop(0, groups)
    def _(g):
        for half in range(2):
            grad_out(half, g).wait()
        each_peer(lambda peer: kv_out(g, peer).wait_send())
        each_peer(lambda peer: [term_out(g, peer, which).wait_send() for which in range(2)])
        if relay:
            for which in range(2):
                for j in range(2):
                    passed(g, which, j).wait_send()
                    relay_out(g, which, j).wait_send()

        @pl.when(section > 0)
        def _():
            for c in range(2):
                dq_out(g, c).wait_send()

        @pl.when(section < sections - 1)
        def _():
            for c in range(2):
                dq_in(g, c).wait_recv()


def spread_kernel(pooled_grads, given, key_grad, value_grad, upstream):
    tokens = given.shape[1]
    shape = (tokens, tokens // 4)
    token = lax.broadcasted_iota(jnp.int32, shape, 0)
    token = jnp.where(token >= tokens // 2, token - tokens // 2, token)
    cell = lax.broadcasted_iota(jnp.int32, shape, 1)
    spread = jnp.where((token >> 1) == cell, 1.0, 0.0).astype(jnp.bfloat16)
    key_grad[0] = dot(spread, pooled_grads[0], ((1,), (0,))).astype(jnp.bfloat16)
    value_grad[0] = dot(spread, pooled_grads[1], ((1,), (0,))).astype(jnp.bfloat16)
    upstream[...] = given[...]


def shards(query, key, value, out_grad, tile_mask):
    _, tokens, width = query.shape
    sections = lax.axis_size("section")
    count = lax.axis_size("ctx")
    pool = tokens // 4
    half_heads = width // HD // 2
    per_group = max(n for n in (1, 2, 3) if half_heads % n == 0)
    groups = half_heads // per_group
    wide = per_group * HD
    any_spec = pl.BlockSpec(memory_space=pltpu.HBM)
    dma = pltpu.SemaphoreType.DMA
    low = jnp.bfloat16
    whole = jax.ShapeDtypeStruct(query.shape, low)
    tiles = tile_mask.shape[1]
    pooled_grads, upstream = pl.pallas_call(
        functools.partial(kernel, sections, count, groups, wide),
        out_shape=(jax.ShapeDtypeStruct((2, pool, width), low), whole),
        in_specs=[any_spec] * 5,
        out_specs=(any_spec,) * 2,
        scratch_shapes=[
            pltpu.VMEM((2, tokens, width), low),
            pltpu.VMEM((2, groups, 2, pool, wide), low),
            pltpu.VMEM((groups, count, 2, pool, wide), low),
            pltpu.VMEM((groups, 2, 2, tokens, wide), low),
            pltpu.VMEM(tile_mask.shape, jnp.int32),
            pltpu.VMEM((2, tiles, tokens), jnp.float32),
            pltpu.VMEM((groups, count, 2, pool, wide), low),
            pltpu.VMEM((groups, count, 2, pool, wide), low),
            pltpu.VMEM((groups, 2, 2, pool, wide), low),
            pltpu.VMEM((groups, 2, tokens, wide), low),
            pltpu.VMEM((2, groups, 2, pool, wide), low),
            dma((2, 2, groups)),
            dma((2, groups)),
            dma,
            dma((2, groups)),
            dma((2, groups)),
            dma((2,)),
            dma((groups, count)),
            dma((groups, count)),
            dma((groups, 2, 2)),
            dma((groups, 2, 2)),
            dma((groups, count, 2)),
            dma((groups, count, 2)),
            dma((groups, 2, 2)),
            dma((groups, 2, 2)),
            dma((groups, 2)),
            dma((groups, 2)),
            dma((2, groups)),
        ],
        compiler_params=pltpu.CompilerParams(
            collective_id=0, has_side_effects=True, vmem_limit_bytes=60 * 1024 * 1024
        ),
    )(query, key, value, out_grad, tile_mask)
    band = min(width, 4 * wide)
    block = pl.BlockSpec((1, tokens, band), lambda i: (0, 0, i))
    return pl.pallas_call(
        spread_kernel,
        grid=(width // band,),
        out_shape=(whole, whole, whole),
        in_specs=[pl.BlockSpec((2, pool, band), lambda i: (0, 0, i)), block],
        out_specs=(block,) * 3,
    )(pooled_grads, upstream)


def solution(mesh):
    spec = P("section", "ctx", None)
    return jax.shard_map(
        shards,
        mesh=mesh,
        in_specs=(spec, spec, spec, spec, P("ctx", None)),
        out_specs=(spec, spec, spec),
        check_vma=False,
    )
```

```python
import functools

import jax
import jax.numpy as jnp
from jax import lax
from jax.experimental import pallas as pl
from jax.experimental.pallas import tpu as pltpu
from jax.sharding import PartitionSpec as P

HD = 128
MESH = pl.DeviceIdType.MESH
LOG2E = 1.4426950408889634
AHEAD = 2


def dot(a, b, dims):
    return lax.dot_general(a, b, (dims, ((), ())), preferred_element_type=jnp.float32)


def kernel(
    sections, count, groups, wide,
    q_hbm, k_hbm, v_hbm, d_hbm, mask_hbm,
    pg_hbm, up_hbm,
    kin, pooled, kv, qd, mask, bias, terms, arrived, relayed, dq, grads,
    in_sem, own_sem, mask_sem, swap_send, swap_recv, bias_sems,
    kv_send, kv_recv, pass_send, pass_recv, term_send, term_recv, relay_send, relay_recv,
    dq_send, dq_recv, out_sem,
):
    tokens = qd.shape[3]
    row_len = tokens // 2
    pool = pooled.shape[3]
    section = lax.axis_index("section")
    me = lax.axis_index("ctx")
    core = lax.rem(me, 2)
    chip_first = me - core
    partner = chip_first + 1 - core
    relay = count == 8
    across = lax.rem(me // 2, 2)
    beside_x = chip_first + 2 - 4 * across
    beside_y = chip_first + 4 - 8 * (me // 4)
    corner = 2 * (count // 2 - 1) - chip_first

    def columns(half, g):
        return pl.ds(pl.multiple_of((half * groups + g) * wide, wide), wide)

    def in_copy(which, half, g):
        src = (k_hbm, v_hbm)[which]
        return pltpu.make_async_copy(
            src.at[0, :, columns(half, g)], kin.at[which, :, columns(half, g)], in_sem.at[which, half, g]
        )

    def own_copy(which, g):
        src = (q_hbm, d_hbm)[which]
        return pltpu.make_async_copy(src.at[0, :, columns(core, g)], qd.at[g, which, core], own_sem.at[which, g])

    def own_mask():
        return pltpu.make_async_copy(mask_hbm, mask, mask_sem)

    @pl.loop(0, groups)
    def _(g):
        for which in range(2):
            for half in range(2):
                in_copy(which, half, g).start()

    @pl.loop(0, groups)
    def _(g):
        for which in range(2):
            own_copy(which, g).start()

    own_mask().start()

    own_mask().wait()
    tile = lax.broadcasted_iota(jnp.int32, (2, tokens), 0)
    token = lax.broadcasted_iota(jnp.int32, (2, tokens), 1)
    inside = jnp.where((token >= row_len) == (tile == 1), 1.0, 0.0)
    reads = dot(mask[...].astype(jnp.float32), inside, ((0,), (0,)))
    bias[core] = jnp.where(reads > 0.5, 0.0, -1e30)

    barrier = pltpu.get_barrier_semaphore()
    for step in range(1, count):
        pl.semaphore_signal(
            barrier, inc=1, device_id=(section, lax.rem(me + step, count)), device_id_type=MESH
        )

    @pl.when(section > 0)
    def _():
        for c in range(2):
            pl.semaphore_signal(barrier, inc=1, device_id=(section - 1, chip_first + c), device_id_type=MESH)

    @pl.when(section < sections - 1)
    def _():
        for c in range(2):
            pl.semaphore_signal(barrier, inc=1, device_id=(section + 1, chip_first + c), device_id_type=MESH)

    edges = jnp.where(section > 0, 2, 0) + jnp.where(section < sections - 1, 2, 0)
    pl.semaphore_wait(barrier, count - 1 + edges)

    def swap(which, g):
        src = (q_hbm, d_hbm)[which]
        return pltpu.make_async_remote_copy(
            src_ref=src.at[0, :, columns(1 - core, g)],
            dst_ref=qd.at[g, which, core],
            send_sem=swap_send.at[which, g],
            recv_sem=swap_recv.at[which, g],
            device_id=(section, partner),
            device_id_type=MESH,
        )

    def swap_bias():
        return pltpu.make_async_remote_copy(
            src_ref=bias.at[core],
            dst_ref=bias.at[core],
            send_sem=bias_sems.at[0],
            recv_sem=bias_sems.at[1],
            device_id=(section, partner),
            device_id_type=MESH,
        )

    def kv_out(g, peer):
        return pltpu.make_async_remote_copy(
            src_ref=pooled.at[lax.rem(peer, 2), g],
            dst_ref=kv.at[g, me],
            send_sem=kv_send.at[g, peer],
            recv_sem=kv_recv.at[g, me],
            device_id=(section, peer),
            device_id_type=MESH,
        )

    def kv_in(g, peer):
        return pltpu.make_async_remote_copy(
            src_ref=pooled.at[core, g],
            dst_ref=kv.at[g, peer],
            send_sem=kv_send.at[g, peer],
            recv_sem=kv_recv.at[g, peer],
            device_id=(section, peer),
            device_id_type=MESH,
        )

    def pool_matrix(shape, token_dim, value):
        token = lax.broadcasted_iota(jnp.int32, shape, token_dim)
        token = jnp.where(token >= row_len, token - row_len, token)
        cell = lax.broadcasted_iota(jnp.int32, shape, 1 - token_dim)
        return jnp.where((token >> 1) == cell, value, 0.0).astype(jnp.bfloat16)

    def passed(g, which, j):
        src = ((beside_x, beside_y)[which]) + j
        dst = ((beside_y, beside_x)[which]) + core
        return pltpu.make_async_remote_copy(
            src_ref=kv.at[g, src, which],
            dst_ref=kv.at[g, src, which],
            send_sem=pass_send.at[g, which, j],
            recv_sem=pass_recv.at[g, which, j],
            device_id=(section, dst),
            device_id_type=MESH,
        )

    def each_peer(act):
        if relay:
            for j in range(2):
                act(beside_x + j)
                act(beside_y + j)
            act(partner)
        else:
            @pl.loop(1, count)
            def _(step):
                act(lax.rem(me + step, count))

    def pool_group(g):
        mean = pool_matrix((pool, tokens), 1, 0.25)
        for half in range(2):
            for which in range(2):
                in_copy(which, half, g).wait()
                block = dot(mean, kin[which, :, columns(half, g)], ((1,), (0,)))
                pooled[half, g, which] = block.astype(jnp.bfloat16)
        kv[g, me] = pooled[core, g]

    def send_group(g):
        each_peer(lambda peer: kv_out(g, peer).start())
        for which in range(2):
            swap(which, g).start()

    def pass_group(g):
        each_peer(lambda peer: kv_in(g, peer).wait_recv())
        if relay:
            for which in range(2):
                for j in range(2):
                    passed(g, which, j).start()

    ahead = min(AHEAD, groups)
    swap_bias().start()
    for g in range(ahead):
        pool_group(g)
        send_group(g)

    @pl.loop(ahead, groups)
    def _(g):
        pool_group(g)

    pass_group(0)

    def term_out(g, peer, which):
        return pltpu.make_async_remote_copy(
            src_ref=terms.at[g, peer, which],
            dst_ref=arrived.at[g, me, which],
            send_sem=term_send.at[g, peer, which],
            recv_sem=term_recv.at[g, me, which],
            device_id=(section, peer),
            device_id_type=MESH,
        )

    def term_in(g, peer, which):
        return pltpu.make_async_remote_copy(
            src_ref=terms.at[g, peer, which],
            dst_ref=arrived.at[g, peer, which],
            send_sem=term_send.at[g, peer, which],
            recv_sem=term_recv.at[g, peer, which],
            device_id=(section, peer),
            device_id_type=MESH,
        )

    def relay_out(g, which, j):
        return pltpu.make_async_remote_copy(
            src_ref=terms.at[g, corner + j, which],
            dst_ref=relayed.at[g, which, j],
            send_sem=relay_send.at[g, which, j],
            recv_sem=relay_recv.at[g, which, j],
            device_id=(section, ((beside_x, beside_y)[which]) + core),
            device_id_type=MESH,
        )

    def combine(g):
        for which in range(2):
            for j in range(2):
                relay_out(g, which, j).wait_recv()
                peer = ((beside_y, beside_x)[which]) + j
                both = terms[g, peer, which].astype(jnp.float32) + relayed[g, which, j].astype(jnp.float32)
                terms[g, peer, which] = both.astype(jnp.bfloat16)
                term_out(g, peer, which).start()

    def send_terms(g):
        if relay:
            for which in range(2):
                for j in range(2):
                    relay_out(g, which, j).start()
            for which in range(2):
                for j in range(2):
                    term_out(g, ((beside_x, beside_y)[which]) + j, which).start()
                term_out(g, partner, which).start()
        else:
            @pl.loop(1, count)
            def _(step):
                for which in range(2):
                    term_out(g, lax.rem(me + step, count), which).start()

    def dq_out(g, c):
        return pltpu.make_async_remote_copy(
            src_ref=dq.at[g, c],
            dst_ref=up_hbm.at[0, :, columns(core, g)],
            send_sem=dq_send.at[g, c],
            recv_sem=dq_recv.at[g, core],
            device_id=(section - 1, chip_first + c),
            device_id_type=MESH,
        )

    def dq_in(g, c):
        return pltpu.make_async_remote_copy(
            src_ref=dq.at[g, c],
            dst_ref=up_hbm.at[0, :, columns(c, g)],
            send_sem=dq_send.at[g, c],
            recv_sem=dq_recv.at[g, c],
            device_id=(section + 1, chip_first + c),
            device_id_type=MESH,
        )

    swap_bias().wait()
    scale = 1.0 / HD**0.5

    @pl.loop(0, groups)
    def _(g):
        for which in range(2):
            own_copy(which, g).wait()
            swap(which, g).wait()

        if relay:
            for which in range(2):
                for j in range(2):
                    passed(g, which, j).wait_recv()

        @pl.when(g + ahead < groups)
        def _():
            send_group(g + ahead)

        for h in range(wide // HD):
            hs = slice(h * HD, (h + 1) * HD)
            k2 = kv[g, :, 0, :, hs].reshape(count * pool, HD)
            v2 = kv[g, :, 1, :, hs].reshape(count * pool, HD)
            dk = dv = None
            for c in range(2):
                qc = qd[g, 0, c, :, hs]
                dc = qd[g, 1, c, :, hs]
                scores = dot(k2, qc, ((1,), (1,))).reshape(count, pool, tokens)
                scores = (scores + bias[c][:, None, :]).reshape(count * pool, tokens)
                top = jnp.max(scores, axis=0, keepdims=True)
                expo = jnp.exp2((scores - top) * (scale * LOG2E))
                probs = expo * (1.0 / jnp.sum(expo, axis=0, keepdims=True))
                low = probs.astype(jnp.bfloat16)
                dprob = dot(v2, dc, ((1,), (1,)))
                delta = jnp.sum(low.astype(jnp.float32) * dprob, axis=0, keepdims=True)
                sgrad = (probs * (dprob - delta) * scale).astype(jnp.bfloat16)
                dkc = dot(sgrad, qc, ((1,), (0,)))
                dvc = dot(low, dc, ((1,), (0,)))
                dk = dkc if dk is None else dk + dkc
                dv = dvc if dv is None else dv + dvc
                dq[g, c, :, hs] = dot(k2, sgrad, ((0,), (0,))).T.astype(jnp.bfloat16)
            terms[g, :, 0, :, hs] = dk.astype(jnp.bfloat16).reshape(count, pool, HD)
            terms[g, :, 1, :, hs] = dv.astype(jnp.bfloat16).reshape(count, pool, HD)
            if h == 0:
                @pl.when(g + 1 < groups)
                def _():
                    pass_group(g + 1)

                if relay:
                    @pl.when(g > 0)
                    def _():
                        combine(g - 1)

        send_terms(g)

        @pl.when(section > 0)
        def _():
            for c in range(2):
                dq_out(g, c).start()

        arrived[g, me] = terms[g, me]

    if relay:
        combine(groups - 1)

    def grad_out(half, g):
        return pltpu.make_async_copy(grads.at[half, g], pg_hbm.at[:, :, columns(half, g)], out_sem.at[half, g])

    @pl.loop(0, groups)
    def _(g):
        each_peer(lambda peer: [term_in(g, peer, which).wait_recv() for which in range(2)])
        for half in range(2):
            if relay:
                peers = [chip_first + half, beside_x + half, beside_y + half]
            else:
                peers = range(half, count, 2)
            for which in range(2):
                total = sum(arrived[g, peer, which].astype(jnp.float32) for peer in peers)
                grads[half, g, which] = (total / 4.0).astype(jnp.bfloat16)
            grad_out(half, g).start()

    @pl.when(section == sections - 1)
    def _():
        qd[0, 0, 0] = jnp.zeros((tokens, wide), jnp.bfloat16)

        def zero_out(g, half):
            return pltpu.make_async_copy(qd.at[0, 0, 0], up_hbm.at[0, :, columns(half, g)], dq_recv.at[g, half])

        for half in range(2):
            for g in range(groups):
                zero_out(g, half).start()
        for half in range(2):
            for g in range(groups):
                zero_out(g, half).wait()

    @pl.loop(0, groups)
    def _(g):
        for half in range(2):
            grad_out(half, g).wait()
        each_peer(lambda peer: kv_out(g, peer).wait_send())
        each_peer(lambda peer: [term_out(g, peer, which).wait_send() for which in range(2)])
        if relay:
            for which in range(2):
                for j in range(2):
                    passed(g, which, j).wait_send()
                    relay_out(g, which, j).wait_send()

        @pl.when(section > 0)
        def _():
            for c in range(2):
                dq_out(g, c).wait_send()

        @pl.when(section < sections - 1)
        def _():
            for c in range(2):
                dq_in(g, c).wait_recv()


def spread_kernel(pooled_grads, given, key_grad, value_grad, upstream):
    tokens = given.shape[1]
    shape = (tokens, tokens // 4)
    token = lax.broadcasted_iota(jnp.int32, shape, 0)
    token = jnp.where(token >= tokens // 2, token - tokens // 2, token)
    cell = lax.broadcasted_iota(jnp.int32, shape, 1)
    spread = jnp.where((token >> 1) == cell, 1.0, 0.0).astype(jnp.bfloat16)
    key_grad[0] = dot(spread, pooled_grads[0], ((1,), (0,))).astype(jnp.bfloat16)
    value_grad[0] = dot(spread, pooled_grads[1], ((1,), (0,))).astype(jnp.bfloat16)
    upstream[...] = given[...]


def shards(query, key, value, out_grad, tile_mask):
    _, tokens, width = query.shape
    sections = lax.axis_size("section")
    count = lax.axis_size("ctx")
    pool = tokens // 4
    half_heads = width // HD // 2
    per_group = max(n for n in (1, 2, 3) if half_heads % n == 0)
    groups = half_heads // per_group
    wide = per_group * HD
    any_spec = pl.BlockSpec(memory_space=pltpu.HBM)
    dma = pltpu.SemaphoreType.DMA
    low = jnp.bfloat16
    whole = jax.ShapeDtypeStruct(query.shape, low)
    tiles = tile_mask.shape[1]
    pooled_grads, upstream = pl.pallas_call(
        functools.partial(kernel, sections, count, groups, wide),
        out_shape=(jax.ShapeDtypeStruct((2, pool, width), low), whole),
        in_specs=[any_spec] * 5,
        out_specs=(any_spec,) * 2,
        scratch_shapes=[
            pltpu.VMEM((2, tokens, width), low),
            pltpu.VMEM((2, groups, 2, pool, wide), low),
            pltpu.VMEM((groups, count, 2, pool, wide), low),
            pltpu.VMEM((groups, 2, 2, tokens, wide), low),
            pltpu.VMEM(tile_mask.shape, jnp.int32),
            pltpu.VMEM((2, tiles, tokens), jnp.float32),
            pltpu.VMEM((groups, count, 2, pool, wide), low),
            pltpu.VMEM((groups, count, 2, pool, wide), low),
            pltpu.VMEM((groups, 2, 2, pool, wide), low),
            pltpu.VMEM((groups, 2, tokens, wide), low),
            pltpu.VMEM((2, groups, 2, pool, wide), low),
            dma((2, 2, groups)),
            dma((2, groups)),
            dma,
            dma((2, groups)),
            dma((2, groups)),
            dma((2,)),
            dma((groups, count)),
            dma((groups, count)),
            dma((groups, 2, 2)),
            dma((groups, 2, 2)),
            dma((groups, count, 2)),
            dma((groups, count, 2)),
            dma((groups, 2, 2)),
            dma((groups, 2, 2)),
            dma((groups, 2)),
            dma((groups, 2)),
            dma((2, groups)),
        ],
        compiler_params=pltpu.CompilerParams(
            collective_id=0, has_side_effects=True, vmem_limit_bytes=60 * 1024 * 1024
        ),
    )(query, key, value, out_grad, tile_mask)
    band = 2 * wide
    block = pl.BlockSpec((1, tokens, band), lambda i: (0, 0, i))
    return pl.pallas_call(
        spread_kernel,
        grid=(width // band,),
        out_shape=(whole, whole, whole),
        in_specs=[pl.BlockSpec((2, pool, band), lambda i: (0, 0, i)), block],
        out_specs=(block,) * 3,
    )(pooled_grads, upstream)


def solution(mesh):
    spec = P("section", "ctx", None)
    return jax.shard_map(
        shards,
        mesh=mesh,
        in_specs=(spec, spec, spec, spec, P("ctx", None)),
        out_specs=(spec, spec, spec),
        check_vma=False,
    )
```
